128 devices in a mesh: dp: 8 (over x, y_hi), expert: 16 (over z, y_lo, core).
Axes of the slice: x: 4, y: 4 (y_hi: 2, y_lo: 2; y = y_hi * 2 + y_lo), z: 4, core: 2. Of those that a mesh axis runs over, the one named last changes fastest.
Arguments:
- tokens: bfloat16 [2048, 6144], P('expert', 'dp'), may hold values from -6 to 6
- expert_ids: int32 [2048, 4], P('expert'), may hold values from 0 to 15, all different within a row; in each aligned block of 128 rows (0 to 127, 128 to 255, ...) at most 48 rows name the same one
- route_weights: float32 [2048, 4], P('expert'), may hold values from 0.2 to 1
- gate_weights: bfloat16 [16, 6144, 2048], P('expert', None, 'dp'), may hold values from -0.078125 to 0.078125
- up_weights: bfloat16 [16, 6144, 2048], P('expert', None, 'dp'), may hold values from -0.078125 to 0.078125
- down_weights: bfloat16 [16, 2048, 6144], P('expert', 'dp'), may hold values from -0.125 to 0.125
- grad_out: bfloat16 [2048, 6144], P('expert', 'dp'), may hold values from -6 to 6
Outputs:
- mixed: bfloat16 [2048, 6144], P('expert', 'dp')
- token_grad: bfloat16 [2048, 6144], P('expert', 'dp')
- route_grad: float32 [2048, 4], P('expert')
- gate_grad: bfloat16 [16, 6144, 2048], P('expert', None, 'dp')
- up_grad: bfloat16 [16, 6144, 2048], P('expert', None, 'dp')
- down_grad: bfloat16 [16, 2048, 6144], P('expert', 'dp')
The draws below stay inside these ranges and needn't reach their ends.
Inputs may be any that keep to these rules, and one draw needn't show every extreme that they name: `expert_ids`: the 4 experts of a token differ; in every block of 128 consecutive tokens (the tokens of one index of the expert axis) no expert is chosen by more than 48 tokens, and some expert is chosen by exactly 48 in some blocks.
All inputs are finite; a program needn't handle non-finite values.
Results may differ from the reference program's by a relative error of at most 0.014.
Values may be sent and summed in bfloat16 or wider, within the bound.
No kernel may reach another device: no remote copies, remote signals or barrier semaphores. Data moves between devices by JAX's collectives and lax.ppermute only.
A program may use at most 192 MiB of HBM per device.

```python
import math
import jax
import jax.numpy as jnp
import numpy as np
from jax import lax

D = 6144
FF = 2048
TOP = 4
TOK_DEV = 128
EXPERTS = 16
SLOT = 48
TOKENS = 2048
N_DP = 8
N_EXPERT = 16


def block_levels(own_key, extent, pieces, least, top_value):
    loudness, own = 1.0, jax.random.fold_in(own_key, 6)
    for position, blocks in pieces:
        heights = jnp.exp(jax.random.uniform(jax.random.fold_in(own, position), (blocks,), jnp.float32, least / len(pieces), top_value / len(pieces)))
        loudness = loudness * jnp.repeat(heights, extent[position] // blocks).reshape([-1 if axis == position else 1 for axis in range(len(extent))])
    return loudness


def routed_block(rng, own, number, rows, count, top, bound, slope):
    order = jax.random.permutation(rng, count)
    crowded, ordinary = load_shares(count, rows * top, bound, slope, True), load_shares(count, rows * top, bound, slope, False)
    places = jnp.arange(count)

    def named(lengths, offset_by):
        used = int((lengths > 0).sum())
        fixed = max(1, used // 4)
        moved = fixed + (places - fixed + offset_by * (used - fixed)) % max(1, count - fixed)
        return jnp.zeros((count,), jnp.int32).at[order[jnp.where(places < fixed, places, moved)]].set(jnp.asarray(lengths, jnp.int32))

    lengths = jnp.where(number % 4 == 0, named(crowded, number // 4), named(ordinary, number - number // 4 - 1))
    mixed = jax.random.permutation(jax.random.fold_in(own, 3), count)
    giver, receiver = mixed[0:count // 2 * 2:2], mixed[1:count // 2 * 2:2]
    slack = jnp.minimum(lengths[giver] - 1, bound - lengths[receiver]) // 2
    slack = jnp.where((giver == order[0]) | (receiver == order[0]) | (lengths[receiver] == 0), 0, jnp.maximum(slack, 0))
    moved = jax.random.randint(jax.random.fold_in(own, 4), (count // 2,), 0, 1 << 20) % (slack + 1)
    lengths = lengths.at[giver].add(-moved).at[receiver].add(moved)
    items = jnp.searchsorted(jnp.cumsum(lengths), jnp.arange(rows * top), side="right").astype(jnp.int32)
    listing = items.reshape(top, rows).T
    listing = listing[jax.random.permutation(jax.random.fold_in(own, 1), rows)]
    offset_by = jax.random.randint(jax.random.fold_in(own, 2), (rows, 1), 0, top)
    return jnp.take_along_axis(listing, (jnp.arange(top)[None, :] + offset_by) % top, axis=1)


def load_shares(count, total, most, slope, full):
    loads = [(1 << 20) // math.isqrt(grade ** slope) + 1 for grade in range(1, count + 1)]
    largest = most if full else min(most, max(-(-total // count), total * loads[0] // sum(loads)))
    least = 1 if total - largest >= count - 1 else 0
    holding, spare = [largest] + [least] * (count - 1), total - largest - least * (count - 1)
    while spare > 0:
        free = [i for i in range(1, count) if holding[i] < largest] or [i for i in range(1, count) if holding[i] < most]
        mass, left = sum([loads[i] for i in free]), spare
        for i in free:
            more = min(most - holding[i], max(1, left * loads[i] // mass), spare)
            holding[i] = holding[i] + more
            spare = spare - more
    return np.array(holding)


def normal_values(rng, shape, spread, reach, split=(), held_as=jnp.bfloat16):
    result = jax.random.normal(rng, shape, jnp.float32) * spread
    if len(split) > 0:
        result = block_levels(rng, shape, split, -0.22, 0.18) * result
    return jnp.clip(result, min=-reach, max=reach).astype(held_as)


def setup_inputs(seed: int = 0) -> dict:
    keys = jax.random.split(jax.random.key(seed), 8)
    tokens = normal_values(keys[0], (TOKENS, D), 1.0, 6.0, ((0, 16), (1, 8)))
    expert_ids_keys = jax.random.split(jax.random.fold_in(keys[1], 1), TOKENS // TOK_DEV)
    expert_ids_turns = jax.random.permutation(jax.random.fold_in(keys[1], 3), TOKENS // TOK_DEV)
    expert_ids = jax.vmap(lambda own, number: routed_block(jax.random.fold_in(keys[1], 2), own, number, TOK_DEV, EXPERTS, TOP, SLOT, 2))(expert_ids_keys, expert_ids_turns).reshape((TOKENS, TOP))
    route_weights = jnp.clip(0.2 + 0.8 * jax.random.uniform(keys[2], (TOKENS, TOP), jnp.float32) ** block_levels(keys[2], (TOKENS, TOP), ((0, 16),), -0.2, 0.2), 0.2, 1.0)
    gate_weights = normal_values(keys[3], (EXPERTS, D, FF), D ** -0.5, 0.078125, ((0, 16), (2, 8)))
    up_weights = normal_values(keys[4], (EXPERTS, D, FF), D ** -0.5, 0.078125, ((0, 16), (2, 8)))
    down_weights = normal_values(keys[5], (EXPERTS, FF, D), FF ** -0.5, 0.125, ((0, 16), (1, 8)))
    grad_out = normal_values(keys[6], (TOKENS, D), 1.0, 6.0, ((0, 16), (1, 8)))
    return dict(tokens=tokens, expert_ids=expert_ids, route_weights=route_weights, gate_weights=gate_weights, up_weights=up_weights, down_weights=down_weights, grad_out=grad_out)


def reference(tokens, expert_ids, route_weights, gate_weights, up_weights, down_weights, grad_out):
    assigned = TOKENS * TOP
    capacity = min(TOKENS, N_EXPERT * SLOT)
    group_width = FF // N_DP
    flat_ids = expert_ids.reshape(assigned)
    scaled = (route_weights[:, :, None] * grad_out[:, None, :].astype(jnp.float32)).astype(jnp.bfloat16).reshape(assigned, D)
    contract_last = (((1,), (1,)), ((), ()))
    contract_first = (((0,), (0,)), ((), ()))

    def expert_step(totals, expert):
        outputs, input_grads = totals
        picked = jnp.nonzero(flat_ids == expert, size=capacity, fill_value=assigned)[0].astype(jnp.int32)
        usable = picked < assigned
        safe_index = jnp.where(usable, picked, 0).astype(jnp.int32)
        inputs = jnp.where(usable[:, None], tokens[safe_index // TOP], jnp.zeros((), jnp.bfloat16))
        gate_weight = gate_weights[expert]
        up_weight = up_weights[expert]
        down_weight = down_weights[expert]
        gate_pre = jnp.dot(inputs, gate_weight, preferred_element_type=jnp.float32)
        up_pre = jnp.dot(inputs, up_weight, preferred_element_type=jnp.float32)
        gate_sigmoid = jax.nn.sigmoid(gate_pre)
        hidden = (gate_pre * gate_sigmoid * up_pre).astype(jnp.bfloat16)
        out_total = jnp.zeros((capacity, D), jnp.float32)
        for group in range(N_DP):
            low = group * group_width
            part = jnp.dot(hidden[:, low:low + group_width], down_weight[low:low + group_width],
                           preferred_element_type=jnp.float32).astype(jnp.bfloat16)
            out_total = out_total + lax.optimization_barrier(part).astype(jnp.float32)
        expert_out = out_total.astype(jnp.bfloat16)
        out_grad = jnp.where(usable[:, None], scaled[safe_index], jnp.zeros((), jnp.bfloat16))
        hidden_grad = lax.dot_general(out_grad, down_weight, contract_last, preferred_element_type=jnp.float32)
        grad_gate_pre = (hidden_grad * up_pre * gate_sigmoid * (1.0 + gate_pre * (1.0 - gate_sigmoid))).astype(jnp.bfloat16)
        grad_up_pre = (hidden_grad * gate_pre * gate_sigmoid).astype(jnp.bfloat16)
        down_grad = lax.dot_general(hidden, out_grad, contract_first, preferred_element_type=jnp.float32).astype(jnp.bfloat16)
        gate_grad = lax.dot_general(inputs, grad_gate_pre, contract_first, preferred_element_type=jnp.float32).astype(jnp.bfloat16)
        up_grad = lax.dot_general(inputs, grad_up_pre, contract_first, preferred_element_type=jnp.float32).astype(jnp.bfloat16)
        row_total = jnp.zeros((capacity, D), jnp.float32)
        for group in range(N_DP):
            low = group * group_width
            part = (lax.dot_general(grad_gate_pre[:, low:low + group_width], gate_weight[:, low:low + group_width],
                                    contract_last, preferred_element_type=jnp.float32)
                    + lax.dot_general(grad_up_pre[:, low:low + group_width], up_weight[:, low:low + group_width],
                                      contract_last, preferred_element_type=jnp.float32)).astype(jnp.bfloat16)
            row_total = row_total + lax.optimization_barrier(part).astype(jnp.float32)
        row_grad = row_total.astype(jnp.bfloat16)
        outputs = outputs.at[picked].set(expert_out, mode="drop")
        input_grads = input_grads.at[picked].set(row_grad, mode="drop")
        return (outputs, input_grads), (gate_grad, up_grad, down_grad)

    initial = (jnp.zeros((assigned, D), jnp.bfloat16), jnp.zeros((assigned, D), jnp.bfloat16))
    (outputs, input_grads), (gate_grad, up_grad, down_grad) = lax.scan(
        expert_step, initial, jnp.arange(EXPERTS, dtype=jnp.int32))
    slot_out = outputs.reshape(TOKENS, TOP, D).astype(jnp.float32)
    mixed = jnp.sum(route_weights[:, :, None] * slot_out, axis=1).astype(jnp.bfloat16)
    route_grad = jnp.sum(slot_out * grad_out[:, None, :].astype(jnp.float32), axis=2)
    token_grad = jnp.sum(input_grads.reshape(TOKENS, TOP, D).astype(jnp.float32), axis=1).astype(jnp.bfloat16)
    return (mixed, token_grad, route_grad, gate_grad, up_grad, down_grad)
```

```python
import functools

import jax
import jax.numpy as jnp
from jax import lax
from jax.experimental import pallas as pl
from jax.experimental.pallas import tpu as pltpu
from jax.sharding import PartitionSpec as P


NX, NY = 4, 2
LAST = (((1,), (1,)), ((), ()))
FIRST = (((0,), (0,)), ((), ()))
BF, F32 = jnp.bfloat16, jnp.float32
RING = (0, -1, 1, 2)


def hop(value, dx, dy=0):
    pairs = [
        (x * NY + y, ((x + dx) % NX) * NY + (y + dy) % NY) for x in range(NX) for y in range(NY)
    ]
    return lax.ppermute(value, "dp", pairs)


def dot(a, b, dims=None):
    if dims is None:
        return jnp.dot(a, b, preferred_element_type=F32)
    return lax.dot_general(a, b, dims, preferred_element_type=F32)


def exchange(rows, experts):
    count, width = rows.shape
    blocks = rows.reshape(experts, count // experts, width)
    return lax.all_to_all(blocks, "expert", split_axis=0, concat_axis=0, tiled=True).reshape(
        count, width
    )


def ring_gather(value):
    half = value.shape[0] // 2
    left = hop(value, 1)
    right = hop(value, -1)
    far_top = hop(left[:half], 1)
    far_low = hop(right[half:], -1)
    return {0: (value,), -1: (left,), 1: (right,), 2: (far_top, far_low)}


def call(body, name, grid, ins, outs, out_shape, scratch, args, scalars, flops):
    size = sum(a.size * a.dtype.itemsize for a in args)
    size += sum(s.size * s.dtype.itemsize for s in out_shape)
    return pl.pallas_call(
        body,
        name=name,
        grid_spec=pltpu.PrefetchScalarGridSpec(
            num_scalar_prefetch=1, grid=(grid,), in_specs=ins, out_specs=outs, scratch_shapes=scratch
        ),
        out_shape=out_shape,
        cost_estimate=pl.CostEstimate(flops=flops, bytes_accessed=size, transcendentals=0),
        compiler_params=pltpu.CompilerParams(vmem_limit_bytes=40 << 20),
    )(scalars, *args)


def whole(shape):
    return pl.BlockSpec(shape, lambda i, s: (0,) * len(shape))


ANY = pl.BlockSpec(memory_space=pl.ANY)


def stage(groups, refs, buf, sem, step):
    def copies(at):
        first = sum(len(g) for g in groups[:at])
        row, out = 0, []
        for j, part in enumerate(groups[at]):
            n = part.shape[0]
            out.append(
                pltpu.make_async_copy(
                    refs[first + j], buf.at[at % 2, pl.ds(row, n)], sem.at[at % 2, j]
                )
            )
            row += n
        return out

    def start(at):
        for c in copies(at):
            c.start()

    for at in range(len(groups)):

        @pl.when(step == at)
        def _(at=at):
            if at == 0:
                start(0)
            if at + 1 < len(groups):
                start(at + 1)
            for c in copies(at):
                c.wait()

    return lax.rem(step, 2)


def gate_up(groups, places, gate_blocks, up_blocks, total):
    rows = sum(p.shape[0] for p in groups[0])
    width, units = gate_blocks.shape[1:]
    parts = [p for g in groups for p in g]
    tile = rows // 3

    def body(s_ref, *refs):
        ins, rest = refs[: len(parts)], refs[len(parts) :]
        g_ref, u_ref = rest[:2]
        out, buf, sem = rest[-3:]
        step = pl.program_id(0)
        slot = stage(groups, ins, buf, sem, step)

        @pl.when(step == 0)
        def _():
            out[...] = jnp.zeros_like(out) if total is None else rest[2][...]

        @pl.loop(0, 3)
        def _(m):
            at = pl.ds(pl.multiple_of(m * tile, tile), tile)
            x = buf[slot, at, :]
            out[at, :units] += dot(x, g_ref[0])
            out[at, units:] += dot(x, u_ref[0])

    block = pl.BlockSpec((1, width, units), lambda i, s: (s[i], 0, 0))
    args = [*parts, gate_blocks, up_blocks] + ([] if total is None else [total])
    ins = [ANY] * len(parts) + [block, block] + ([] if total is None else [whole(total.shape)])
    return call(
        body, "gate_up", len(groups), ins, [whole((rows, 2 * units))],
        [jax.ShapeDtypeStruct((rows, 2 * units), F32)],
        [pltpu.VMEM((2, rows, width), BF), pltpu.SemaphoreType.DMA((2, 2))],
        args, jnp.stack(places), 4 * len(groups) * rows * width * units,
    )[0]


def weight_grads(groups, places, grad_gate, grad_up):
    rows, units = grad_gate.shape
    width = groups[0][0].shape[1]
    parts = [p for g in groups for p in g]
    tile = width // 3

    def body(s_ref, *refs):
        ins = refs[: len(parts)]
        gg, gu, out_g, out_u, buf, sem = refs[len(parts) :]
        slot = stage(groups, ins, buf, sem, pl.program_id(0))

        @pl.loop(0, 3)
        def _(m):
            at = pl.ds(pl.multiple_of(m * tile, tile), tile)
            x = buf[slot, :, at]
            out_g[0, at, :] = dot(x, gg[...], FIRST).astype(BF)
            out_u[0, at, :] = dot(x, gu[...], FIRST).astype(BF)

    block = pl.BlockSpec((1, width, units), lambda i, s: (s[i], 0, 0))
    shape = jax.ShapeDtypeStruct((len(groups), width, units), BF)
    return call(
        body, "weight_grads", len(groups), [ANY] * len(parts) + [whole((rows, units))] * 2,
        [block, block], [shape, shape],
        [pltpu.VMEM((2, rows, width), BF), pltpu.SemaphoreType.DMA((2, 2))],
        [*parts, grad_gate, grad_up], jnp.stack(places), 4 * len(groups) * rows * width * units,
    )


def row_part(grad_gate, grad_up, gate_blocks, up_blocks, place, tiles, adds):
    rows, units = grad_gate.shape
    width = gate_blocks.shape[1]
    tile = rows // 4
    lo, hi = tiles

    def body(s_ref, gg, gu, g_ref, u_ref, *refs):
        out = refs[-1]
        value = dot(gg[...], g_ref[0], LAST) + dot(gu[...], u_ref[0], LAST)
        step = pl.program_id(0) + lo
        for (array, first), ref in zip(adds, refs, strict=False):
            count = array.shape[0] // tile
            inside = (step >= first) & (step < first + count)
            more = ref[...].astype(F32)
            value = value + (more if count == hi - lo else jnp.where(inside, more, 0.0))
        out[...] = value.astype(BF)

    rowed = pl.BlockSpec((tile, units), lambda i, s: (i + lo, 0))
    block = pl.BlockSpec((1, width, units), lambda i, s: (s[0], 0, 0))

    def add_spec(array, first):
        last = array.shape[0] // tile - 1
        return pl.BlockSpec((tile, width), lambda i, s: (jnp.clip(i + lo - first, 0, last), 0))

    return call(
        body, "row_part", hi - lo, [rowed, rowed, block, block] + [add_spec(*a) for a in adds],
        [pl.BlockSpec((tile, width), lambda i, s: (i, 0))],
        [jax.ShapeDtypeStruct(((hi - lo) * tile, width), BF)], [],
        [grad_gate, grad_up, gate_blocks, up_blocks] + [a for a, _ in adds],
        place[None], 4 * (hi - lo) * tile * width * units,
    )[0]


def split_columns(wide, places, width):
    count = len(places)

    def body(s_ref, x, *outs):
        for j in range(count):

            @pl.when(pl.program_id(0) == j)
            def _(j=j):
                outs[j][...] = x[...]

    shape = (wide.shape[0], width)
    return call(
        body, "split_columns", count, [pl.BlockSpec(shape, lambda i, s: (0, s[i]))],
        [whole(shape)] * count, [jax.ShapeDtypeStruct(shape, wide.dtype)] * count, [],
        [wide], jnp.stack(places), 0,
    )


def join_columns(blocks, places):
    count = len(blocks)
    shape = blocks[0].shape

    def body(s_ref, *refs):
        for j in range(count):

            @pl.when(pl.program_id(0) == j)
            def _(j=j):
                refs[-1][...] = refs[j][...]

    return call(
        body, "join_columns", count, [whole(shape)] * count,
        [pl.BlockSpec(shape, lambda i, s: (0, s[i]))],
        [jax.ShapeDtypeStruct((shape[0], shape[1] * count), BF)], [],
        list(blocks), jnp.stack(places), 0,
    )[0]


def hidden_parts(grads, blocks, dtype):
    rows, width = grads.shape
    units = blocks[0].shape[0]
    groups = [(b,) for b in blocks]
    tile = rows // 3

    def body(s_ref, *refs):
        x, out, buf, sem = refs[len(blocks) :]
        slot = stage(groups, refs[: len(blocks)], buf, sem, pl.program_id(0))

        @pl.loop(0, 3)
        def _(m):
            at = pl.ds(pl.multiple_of(m * tile, tile), tile)
            out[at, :] = dot(x[at, :], buf[slot], LAST).astype(dtype)

    return call(
        body, "hidden_parts", len(blocks), [ANY] * len(blocks) + [whole((rows, width))],
        [pl.BlockSpec((rows, units), lambda i, s: (0, i))],
        [jax.ShapeDtypeStruct((rows, units * len(blocks)), dtype)],
        [pltpu.VMEM((2, units, width), BF), pltpu.SemaphoreType.DMA((2, 1))],
        [*blocks, grads], jnp.zeros((1,), jnp.int32), 2 * len(blocks) * rows * width * units,
    )[0]


def expert_outputs(hidden_groups, block_groups):
    rows = sum(p.shape[0] for p in hidden_groups[0])
    units2 = hidden_groups[0][0].shape[1]
    width = block_groups[0][0].shape[1]
    hid = [p for g in hidden_groups for p in g]
    blocks = [p for g in block_groups for p in g]
    tile = rows // 3
    count = len(hidden_groups)

    def body(s_ref, *refs):
        a = refs[: len(hid)]
        b = refs[len(hid) : len(hid) + len(blocks)]
        out, total, hbuf, wbuf, hsem, wsem = refs[len(hid) + len(blocks) :]
        step = pl.program_id(0)
        slot = stage(hidden_groups, a, hbuf, hsem, step)
        stage(block_groups, b, wbuf, wsem, step)

        @pl.when(step == 0)
        def _():
            total[...] = jnp.zeros_like(total)

        @pl.loop(0, 3)
        def _(m):
            at = pl.ds(pl.multiple_of(m * tile, tile), tile)
            total[at, :] += dot(hbuf[slot, at, :], wbuf[slot])

        @pl.when(step == count - 1)
        def _():
            out[...] = total[...].astype(BF)

    return call(
        body, "expert_outputs", count, [ANY] * (len(hid) + len(blocks)),
        [whole((rows, width))], [jax.ShapeDtypeStruct((rows, width), BF)],
        [pltpu.VMEM((rows, width), F32), pltpu.VMEM((2, rows, units2), BF),
         pltpu.VMEM((2, units2, width), BF), pltpu.SemaphoreType.DMA((2, 2)), pltpu.SemaphoreType.DMA((2, 2))],
        hid + blocks, jnp.zeros((1,), jnp.int32), 2 * count * rows * width * units2,
    )[0]


def shards(tokens, expert_ids, route_weights, gate_weights, up_weights, down_weights, grad_out):
    experts = lax.axis_size("expert")
    count, width = tokens.shape
    top = expert_ids.shape[1]
    slot = min(count, 3 * count * top // (2 * experts))
    rows = experts * slot
    half = rows // 2
    place = lax.axis_index("dp")
    my_x, my_y = place // NY, place % NY

    def index(dx, dy):
        return ((my_x + dx) % NX) * NY + (my_y + dy) % NY

    gate_blocks = gate_weights[0].reshape(NX * NY, width, -1)
    up_blocks = up_weights[0].reshape(NX * NY, width, -1)
    units = gate_blocks.shape[2]
    around = [(dx, dy) for dy in range(NY) for dx in range(NX)]

    tokens_pair = hop(tokens, 0, 1)
    chosen = expert_ids[:, :, None] == jnp.arange(experts, dtype=jnp.int32)[None, None, :]
    picks = jnp.any(chosen, axis=1).astype(BF)
    before = (jnp.arange(count)[:, None] > jnp.arange(count)[None, :]).astype(BF)
    earlier = dot(before, picks)
    rank = jnp.sum(jnp.where(chosen, earlier[:, None, :], 0.0), axis=2).astype(jnp.int32)
    positions = expert_ids * slot + rank
    hits = [
        jnp.arange(rows, dtype=jnp.int32)[:, None] == positions[:, k][None, :] for k in range(top)
    ]
    by_token = sum(h.astype(F32) for h in hits).astype(BF)
    weighted = sum(jnp.where(h, route_weights[:, k][None, :], 0.0) for k, h in enumerate(hits))
    slot_weight = jnp.sum(weighted, axis=1)

    own = exchange(dot(by_token, tokens).astype(BF), experts)
    grads = exchange((dot(by_token, grad_out) * slot_weight[:, None]).astype(BF), experts)
    pair = exchange(dot(by_token, tokens_pair).astype(BF), experts)

    blocks = split_columns(down_weights[0], [index(-dx, dy) for dx, dy in around], width)
    down = {}
    for (dx, dy), block in zip(around, blocks, strict=True):
        down[dx, dy] = hop(block, -dx, dy) if dx or dy else block

    first = ring_gather(own)
    second = ring_gather(pair)
    pre = gate_up(
        [first[dx] for dx in (0, -1, 1)], [index(dx, 0) for dx in (0, -1, 1)],
        gate_blocks, up_blocks, None,
    )
    pre = gate_up(
        [first[2]] + [second[dx] for dx in (0, -1, 1)],
        [index(2, 0)] + [index(dx, 1) for dx in (0, -1, 1)],
        gate_blocks, up_blocks, pre,
    )
    pre = gate_up([second[2]], [index(2, 1)], gate_blocks, up_blocks, pre)

    away = hidden_parts(grads, [down[dx, 1] for dx in range(NX)], BF)
    back = hop(away, 0, 1)
    near = hidden_parts(grads, [down[dx, 0] for dx in range(NX)], F32)

    def hidden_sum(dx):
        at = (dx % NX) * units
        return near[:, at : at + units] + back[:, at : at + units].astype(F32)

    far = hidden_sum(2).astype(BF)
    far_top = hop(far[:half], 1).astype(F32)
    far_low = hop(far[half:], -1).astype(F32)
    to_right = hidden_sum(1) + jnp.pad(far_top, ((0, half), (0, 0)))
    to_left = hidden_sum(-1) + jnp.pad(far_low, ((half, 0), (0, 0)))
    from_left = hop(to_right.astype(BF), 1).astype(F32)
    from_right = hop(to_left.astype(BF), -1).astype(F32)
    hidden_grad = hidden_sum(0) + from_left + from_right

    gate_pre, up_pre = pre[:, :units], pre[:, units:]
    gate_sigmoid = jax.nn.sigmoid(gate_pre)
    hidden = (gate_pre * gate_sigmoid * up_pre).astype(BF)
    grad_gate_pre = (
        hidden_grad * up_pre * gate_sigmoid * (1.0 + gate_pre * (1.0 - gate_sigmoid))
    ).astype(BF)
    grad_up_pre = (hidden_grad * gate_pre * gate_sigmoid).astype(BF)
    route_part = jnp.sum(hidden.astype(F32) * hidden_grad, axis=1)

    def token_sum(dy):
        term = functools.partial(row_part, grad_gate_pre, grad_up_pre, gate_blocks, up_blocks)
        top_half = hop(term(index(2, dy), (0, 2), []), 1)
        low_half = hop(term(index(2, dy), (2, 4), []), -1)
        left = hop(term(index(1, dy), (0, 4), [(top_half, 0)]), 1)
        right = hop(term(index(-1, dy), (0, 4), [(low_half, 2)]), -1)
        summed = term(index(0, dy), (0, 4), [(left, 0), (right, 0)])
        return dot(by_token, exchange(summed, experts), FIRST)

    other_half = hop(token_sum(1).astype(BF), 0, 1)
    token_grad = (token_sum(0) + other_half.astype(F32)).astype(BF)

    route_back = exchange(route_part[:, None], experts)
    route_scaled = jnp.stack(
        [jnp.sum(jnp.where(h, route_back, 0.0), axis=0) for h in hits], axis=1
    )
    route_scaled = route_scaled + hop(route_scaled, 0, 1)
    for step in (1, 2):
        pairs = [(x * NY + y, (x ^ step) * NY + y) for x in range(NX) for y in range(NY)]
        route_scaled = route_scaled + lax.ppermute(route_scaled, "dp", pairs)
    route_grad = route_scaled / route_weights

    hidden_pair = jnp.concatenate([hidden, hop(hidden, 0, 1)], axis=1)
    hidden_all = ring_gather(hidden_pair)
    expert_out = expert_outputs(
        [hidden_all[dx] for dx in RING], [[down[dx % NX, dy] for dy in range(NY)] for dx in RING]
    )
    back_out = exchange(expert_out, experts)
    high = lax.reduce_precision(weighted, 8, 7)
    mixed = dot(high.astype(BF), back_out, FIRST) + dot((weighted - high).astype(BF), back_out, FIRST)
    mixed = mixed.astype(BF)

    gate_grad, up_grad = weight_grads(
        [first[dx] for dx in RING] + [second[dx] for dx in RING],
        [index(dx, dy) for dy in range(NY) for dx in RING],
        grad_gate_pre, grad_up_pre,
    )
    down_parts, places = [], []
    for dx in RING:
        rows_dx = hidden_all[dx]
        block = rows_dx[0] if len(rows_dx) == 1 else jnp.concatenate(rows_dx, axis=0)
        for dy in range(NY):
            grad = dot(block[:, dy * units : (dy + 1) * units], grads, FIRST).astype(BF)
            down_parts.append(hop(grad, dx, dy) if dx or dy else grad)
            places.append(index(-dx, dy))
    down_grad = join_columns(down_parts, places)
    return (
        mixed,
        token_grad,
        route_grad,
        gate_grad.reshape(1, -1, units),
        up_grad.reshape(1, -1, units),
        down_grad[None],
    )


def solution(mesh):
    sharded = P("expert", "dp")
    columns, depth = P("expert", None, "dp"), P("expert", "dp", None)
    in_specs = (sharded, P("expert", None), P("expert", None), columns, columns, depth, sharded)
    out_specs = (sharded, sharded, P("expert", None), columns, columns, depth)
    return jax.shard_map(shards, mesh=mesh, in_specs=in_specs, out_specs=out_specs, check_vma=False)
```
